32 devices in a mesh: replica: 8 (over z, y), fsdp: 4 (over x, core).
Axes of the slice: x: 2, y: 2, z: 4, core: 2. Of those that a mesh axis runs over, the one named last changes fastest.
Arguments:
- inner_weights: bfloat16 [8, 4, 1024, 8192], P('replica', None, 'fsdp'), may hold values from -6 to 6
- snapshot: bfloat16 [1024, 8192], P('fsdp'), may hold values from -6 to 6
- momentum: float32 [1024, 8192], P('fsdp', 'replica'), may hold values from -6 to 6
- rand_bits: int32 [8, 1024, 8192], P('replica', 'fsdp'), may hold values from 0 to 4095
- fragment: int32 [1], replicated, may hold values from 0 to 3
Outputs:
- new_snapshot: bfloat16 [1024, 8192], P('fsdp')
- new_momentum: float32 [1024, 8192], P('fsdp', 'replica')
- new_inner: bfloat16 [8, 4, 1024, 8192], P('replica', None, 'fsdp')
The draws below stay inside these ranges and needn't reach their ends.
Inputs may be any that keep to these rules, and one draw needn't show every extreme that they name: fragment[0] is one of 0, 1, 2, 3, the fragment of the window that syncs.
All inputs are finite; a program needn't handle non-finite values.
Results may differ from the reference program's by a relative error of at most 0.0075.
Values may be sent and summed in bfloat16 or wider, within the bound.
A program may use at most 128 MiB of HBM per device.

```python
import jax
import jax.numpy as jnp
from jax import lax

D = 8192
KV = 1024
FRAGS = 4
REPLICAS = 8


def touch_ends(result, stream_key, smallest, high):
    longest = result.shape.index(max(result.shape))
    spots = []
    for shift in (0, 1):
        where = [jax.random.randint(jax.random.fold_in(stream_key, axis), (), 0, length) for axis, length in enumerate(result.shape)]
        where[longest] = (where[longest] + shift) % result.shape[longest]
        spots.append(tuple(where))
    return result.at[spots[0]].set(smallest).at[spots[1]].set(high)


def level_of(rng, dims, cuts, smallest, high):
    def one(position, parts):
        steps = jax.random.uniform(jax.random.fold_in(jax.random.fold_in(rng, 6), position), (parts,), jnp.float32, smallest / len(cuts), high / len(cuts))
        return jnp.repeat(jnp.exp(steps), dims[position] // parts).reshape((-1,) + (1,) * (len(dims) - position - 1))

    gain = one(*cuts[0])
    for cut in cuts[1:]:
        gain = gain * one(*cut)
    return gain


def gaussian(rng, extent, width, limit, split=(), kind=jnp.bfloat16):
    level = level_of(rng, extent, split, -0.22, 0.18) if split else 1.0
    result = jax.random.normal(rng, extent, jnp.float32) * width * level
    return jnp.minimum(jnp.maximum(result, -limit), limit).astype(kind)


def setup_inputs(seed: int = 0) -> dict:
    seeds = jax.random.split(jax.random.key(seed), 6)
    inner_weights = gaussian(seeds[0], (REPLICAS, FRAGS, KV, D), 1.0, 6.0, ((0, 8), (2, 4)))
    snapshot = gaussian(seeds[1], (KV, D), 1.0, 6.0, ((0, 4),))
    momentum = gaussian(seeds[2], (KV, D), 1.0, 6.0, ((0, 4), (1, 8)), jnp.float32)
    rand_bits = touch_ends(jax.random.randint(seeds[3], (REPLICAS, KV, D), 0, 4096), jax.random.fold_in(seeds[3], 1), 0, 4095).astype(jnp.int32)
    fragment = jax.random.randint(seeds[4], (1,), 0, FRAGS).astype(jnp.int32)
    return {"inner_weights": inner_weights, "snapshot": snapshot, "momentum": momentum, "rand_bits": rand_bits, "fragment": fragment}


momentum_coef = 0.9
outer_rate = 0.7
blend_keep = 0.5
grid_scale = 4.0
bit_levels = 4096.0


def stochastic_grid(snapshot, chosen, rand_bits):
    scaled = grid_scale * (snapshot.astype(jnp.float32) - chosen.astype(jnp.float32))
    lower = jnp.floor(scaled)
    raised = jnp.where(rand_bits.astype(jnp.float32) < bit_levels * (scaled - lower), 1.0, 0.0).astype(jnp.float32)
    return ((lower + raised) / grid_scale).astype(jnp.bfloat16)


def reference(inner_weights, snapshot, momentum, rand_bits, fragment):
    fragment_id = fragment[0].astype(jnp.int32)
    chosen_all = lax.dynamic_index_in_dim(inner_weights, fragment_id, 1, keepdims=False)

    def accumulate(summed, pair):
        chosen, bits = pair
        return summed + stochastic_grid(snapshot, chosen, bits).astype(jnp.float32), None

    summed, _ = lax.scan(accumulate, jnp.zeros(snapshot.shape, jnp.float32), (chosen_all, rand_bits))
    grad = summed / REPLICAS
    new_momentum = momentum_coef * momentum + grad
    new_snapshot = (snapshot.astype(jnp.float32) - outer_rate * (grad + momentum_coef * new_momentum)).astype(jnp.bfloat16)
    blended = (blend_keep * chosen_all.astype(jnp.float32) + (1.0 - blend_keep) * new_snapshot.astype(jnp.float32)[None]).astype(jnp.bfloat16)
    picked = lax.broadcasted_iota(jnp.int32, (1, FRAGS, 1, 1), 1) == fragment_id
    new_inner = jnp.where(picked, blended[:, None], inner_weights)
    return new_snapshot, new_momentum, new_inner
```

```python
import functools

import jax
import jax.numpy as jnp
from jax import lax
from jax.experimental import pallas as pl
from jax.experimental.pallas import tpu as pltpu
from jax.sharding import PartitionSpec as P

momentum_coef = 0.9
outer_rate = 0.7
blend_keep = 0.5
grid_scale = 4.0
bit_levels = 4096.0
MESH = pl.DeviceIdType.MESH
CHUNK_ROWS = 16
OLDEST_FIRST = True
EXCHANGE_VMEM = 30 << 20
FINISH_VMEM = 10 << 20


def when(cond):
    if isinstance(cond, bool):
        return (lambda f: f()) if cond else (lambda f: None)
    return pl.when(cond)


def grid_of(n):
    inner = max(k for k in range(1, n + 1) if n % k == 0 and k * k <= n)
    return n // inner, inner


class Part:
    def __init__(self, bufs, sems, line1, line2, me, cols, width):
        self.own, self.r1, self.l1, self.r2, self.l2, self.res = bufs
        (self.s1, self.sr1, self.sl1, self.s2, self.sr2, self.sl2,
         self.g2, self.g2r, self.g2l, self.g1, self.g1r, self.g1l) = sems
        (self.p1, self.n1, self.d1) = line1
        (self.p2, self.n2, self.d2) = line2
        self.me, self.cols, self.width = me, cols, width
        self.top = self.n1 + self.n2 - 2
        self.last = 2 * self.top
        self.draining = False

    def send(self, src, dst, send_sem, recv_sem, delta):
        copy = pltpu.make_async_remote_copy(
            src_ref=src, dst_ref=dst, send_sem=send_sem, recv_sem=recv_sem,
            device_id={"replica": self.me + delta}, device_id_type=MESH,
        )
        if self.draining:
            copy.wait_send()
        else:
            copy.start()

    def arrive(self, dst, recv_sem):
        if not self.draining:
            pltpu.make_async_remote_copy(
                src_ref=dst, dst_ref=dst, send_sem=recv_sem, recv_sem=recv_sem,
                device_id={"replica": self.me}, device_id_type=MESH,
            ).wait_recv()

    def add1(self, c, q, recv):
        if not self.draining:
            for i in range(self.n2):
                self.own[c, q, i] = self.own[c, q, i] + recv[c, q, i]

    def add2(self, c, q, recv):
        if not self.draining:
            self.own[c, self.p1, q] = self.own[c, self.p1, q] + recv[c, q]

    def send1(self, c, q, right):
        recv, sem, delta = (self.r1, self.sr1, self.d1) if right else (self.l1, self.sl1, -self.d1)
        self.send(self.own.at[c, q], recv.at[c, q], self.s1.at[c, q], sem.at[c, q], delta)

    def send2(self, c, q, right):
        recv, sem, delta = (self.r2, self.sr2, self.d2) if right else (self.l2, self.sl2, -self.d2)
        self.send(self.own.at[c, self.p1, q], recv.at[c, q], self.s2.at[c, q], sem.at[c, q], delta)

    def gsend2(self, c, q, right):
        sem, delta = (self.g2r, self.d2) if right else (self.g2l, -self.d2)
        block = self.res.at[c, self.p1, q]
        self.send(block, block, sem.at[c, q], self.g2.at[c, q], delta)

    def gsend1(self, c, q1, q2, right):
        sem, delta = (self.g1r, self.d1) if right else (self.g1l, -self.d1)
        block = self.res.at[c, q1, q2]
        self.send(block, block, sem.at[c, q1, q2], self.g1.at[c, q1, q2], delta)

    def spread1(self, c, q2):
        p1 = self.p1
        when(p1 < self.n1 - 1)(lambda: self.gsend1(c, p1, q2, True))
        when(p1 > 0)(lambda: self.gsend1(c, p1, q2, False))

    def reduce_line(self, c, h, p, n, send, arrived, recvs, sems, add):
        right_recv, left_recv = recvs
        right_sem, left_sem = sems

        @when(p == h)
        def _():
            for q in range(n - 1, h - (h > 0), -1):
                if h > 0:
                    self.arrive(right_recv.at[c, q], right_sem.at[c, q])
                    if q > h or arrived:
                        add(c, q, right_recv)
                if q > h:
                    send(c, q, True)

        e = n - 1 - h

        @when(p == e)
        def _():
            for q in range(0, e + (h > 0)):
                if h > 0:
                    self.arrive(left_recv.at[c, q], left_sem.at[c, q])
                    if q < e or arrived:
                        add(c, q, left_recv)
                if q < e:
                    send(c, q, False)

    def hop1(self, s, c):
        if s < self.n1:
            self.reduce_line(c, s, self.p1, self.n1, self.send1, True, (self.r1, self.l1), (self.sr1, self.sl1), self.add1)

    def hop2(self, s, c):
        h = s - (self.n1 - 1)
        if 0 <= h < self.n2:
            self.reduce_line(c, h, self.p2, self.n2, self.send2, False, (self.r2, self.l2), (self.sr2, self.sl2), self.add2)

    def update(self, c, snap, mom, mom_next, acc, replicas, share):
        p1, p2 = self.p1, self.p2
        if not self.draining:
            acc[...] = self.own[c, p1, p2].astype(jnp.float32)

            @when(p2 > 0)
            def _():
                acc[...] += self.r2[c, p2].astype(jnp.float32)

            @when(p2 < self.n2 - 1)
            def _():
                acc[...] += self.l2[c, p2].astype(jnp.float32)

            start = self.me * share + self.cols
            if not isinstance(start, int):
                start = pl.multiple_of(start, 128)
            here = pl.ds(self.cols, self.width)
            grad = acc[...] / replicas
            moment = momentum_coef * mom[c, :, here] + grad
            mom_next[c, :, here] = moment
            base = snap[c, :, pl.ds(start, self.width)].astype(jnp.float32)
            self.res[c, p1, p2] = (base - outer_rate * (grad + momentum_coef * moment)).astype(jnp.bfloat16)
        when(p2 < self.n2 - 1)(lambda: self.gsend2(c, p2, True))
        when(p2 > 0)(lambda: self.gsend2(c, p2, False))
        self.spread1(c, p2)

    def gather(self, s, c):
        g = s - self.top
        p1, n1, p2, n2 = self.p1, self.n1, self.p2, self.n2
        if 1 <= g < n2:
            @when(p2 >= g)
            def _():
                self.arrive(self.res.at[c, p1, p2 - g], self.g2.at[c, p2 - g])
                when(p2 < n2 - 1)(lambda: self.gsend2(c, p2 - g, True))
                self.spread1(c, p2 - g)

            @when(p2 + g < n2)
            def _():
                self.arrive(self.res.at[c, p1, p2 + g], self.g2.at[c, p2 + g])
                when(p2 > 0)(lambda: self.gsend2(c, p2 + g, False))
                self.spread1(c, p2 + g)

        for h in range(n2):
            k = g - h
            if not 1 <= k < n1:
                continue
            for side in ((-1, 1) if h else (1,)):
                q2 = p2 + side * h

                @when(q2 >= 0 if side < 0 else q2 < n2)
                def _():
                    @when(p1 >= k)
                    def _():
                        self.arrive(self.res.at[c, p1 - k, q2], self.g1.at[c, p1 - k, q2])
                        when(p1 < n1 - 1)(lambda: self.gsend1(c, p1 - k, q2, True))

                    @when(p1 + k < n1)
                    def _():
                        self.arrive(self.res.at[c, p1 + k, q2], self.g1.at[c, p1 + k, q2])
                        when(p1 > 0)(lambda: self.gsend1(c, p1 + k, q2, False))


def exchange_kernel(dims, frag, inner, snapshot, momentum, bits, inner_v, res_a, res_b, mom_next, *scratch):
    outer, inner_n, chunks, share, wide = dims
    replicas = outer * inner_n
    frags = inner_v.shape[0]
    bbuf, snap, mom, acc_a, acc_b, wsem, bsem, ssem, msem = scratch[:9]
    bufs_a, bufs_b = (*scratch[9:14], res_a), (*scratch[14:19], res_b)
    sems_a, sems_b = scratch[19:31], scratch[31:43]
    me = lax.axis_index("replica")
    y, z = lax.rem(me, inner_n), lax.div(me, inner_n)
    line_y, line_z = (y, inner_n, 1), (z, outer, inner_n)
    part_a = Part(bufs_a, sems_a, line_y, line_z, me, 0, wide)
    part_b = Part(bufs_b, sems_b, line_z, line_y, me, wide, share - wide)
    parts = (part_a, part_b)

    def loads(c, slot):
        return (
            pltpu.make_async_copy(inner.at[0, :, c], inner_v.at[:, c], wsem.at[c]),
            pltpu.make_async_copy(bits.at[c], bbuf.at[slot], bsem.at[slot]),
            pltpu.make_async_copy(snapshot.at[c], snap.at[c], ssem.at[c]),
        )

    for copy in loads(0, 0):
        copy.start()
    mom_copy = pltpu.make_async_copy(momentum, mom, msem)
    mom_copy.start()

    barrier = pltpu.get_barrier_semaphore()
    count = 0
    for pos, n, step in (line_y, line_z):
        for delta, there in ((-step, pos > 0), (step, pos < n - 1)):
            @pl.when(there)
            def _():
                pl.semaphore_signal(barrier, inc=1, device_id={"replica": me + delta}, device_id_type=MESH)

            count = count + there.astype(jnp.int32)
    pl.semaphore_wait(barrier, count)
    mom_copy.wait()

    def round_chunk(c):
        slot = lax.rem(c, 2)

        @pl.when(c + 1 < chunks)
        def _():
            for copy in loads(c + 1, 1 - slot):
                copy.start()

        for copy in loads(c, slot):
            copy.wait()
        which = frag[0]
        for b in range(replicas):
            cols = slice(b * share, (b + 1) * share)
            chosen = inner_v[0, c, :, cols].astype(jnp.float32)
            for f in range(1, frags):
                chosen = jnp.where(which == f, inner_v[f, c, :, cols].astype(jnp.float32), chosen)
            scaled = grid_scale * (snap[c, :, cols].astype(jnp.float32) - chosen)
            lower = jnp.floor(scaled)
            raised = jnp.where(bbuf[slot, :, cols].astype(jnp.float32) < bit_levels * (scaled - lower), 1.0, 0.0)
            rounded = ((lower + raised) / grid_scale).astype(jnp.bfloat16)
            bz, by = b // inner_n, b % inner_n
            part_a.own[c, by, bz] = rounded[:, :wide]
            part_b.own[c, bz, by] = rounded[:, wide:]

    def stage(s, c):
        if s == 0 and not part_a.draining:
            round_chunk(c)
        for part in parts:
            part.hop1(s, c)
            part.hop2(s, c)
        if s == part_a.top:
            part_a.update(c, snap, mom, mom_next, acc_a, replicas, share)
            part_b.update(c, snap, mom, mom_next, acc_b, replicas, share)
        for part in parts:
            part.gather(s, c)

    stages = part_a.last + 1
    order = list(range(stages))
    if OLDEST_FIRST:
        order.reverse()

    def tick(t, carry):
        for s in order:
            c = t - s

            @pl.when(jnp.logical_and(c >= 0, c < chunks))
            def _():
                stage(s, c)

        return carry

    lax.fori_loop(0, chunks + stages - 1, tick, 0)

    part_a.draining = part_b.draining = True

    def drain(c, carry):
        for s in range(stages):
            stage(s, c)
        return carry

    lax.fori_loop(0, chunks, drain, 0)


def finish_kernel(frag, inner_v, res_a, res_b, mom_next, snap_out, mom_out, inner_out, snap_v, blend_v, mom_sem, pass_sem, snap_sem, blend_sem):
    frags, chunks = inner_v.shape[:2]
    n_y, n_z = res_a.shape[1], res_a.shape[2]
    wide = res_a.shape[4]
    share = wide + res_b.shape[4]
    which = frag[0]
    waits = [pltpu.make_async_copy(mom_next, mom_out, mom_sem)]
    for j in range(1, frags):
        other = lax.rem(which + j, frags)
        waits.append(pltpu.make_async_copy(inner_v.at[other], inner_out.at[0, other], pass_sem.at[j]))

    def puts(c):
        return (
            pltpu.make_async_copy(snap_v.at[c], snap_out.at[c], snap_sem.at[c]),
            pltpu.make_async_copy(blend_v.at[c], inner_out.at[0, which, c], blend_sem.at[c]),
        )

    for copy in waits:
        copy.start()

    def blend(c, carry):
        for bz in range(n_z):
            for by in range(n_y):
                first = (bz * n_y + by) * share
                for col, part in ((first, res_a[c, by, bz]), (first + wide, res_b[c, bz, by])):
                    cols = slice(col, col + part.shape[1])
                    snap_v[c, :, cols] = part
                    blend_v[c, :, cols] = (
                        blend_keep * inner_v[which, c, :, cols].astype(jnp.float32)
                        + (1.0 - blend_keep) * part.astype(jnp.float32)
                    ).astype(jnp.bfloat16)
        for copy in puts(c):
            copy.start()
        return carry

    lax.fori_loop(0, chunks, blend, 0)
    for copy in waits:
        copy.wait()

    def settle(c, carry):
        for copy in puts(c):
            copy.wait()
        return carry

    lax.fori_loop(0, chunks, settle, 0)


def body(inner_weights, snapshot, momentum, rand_bits, fragment):
    n = lax.axis_size("replica")
    outer, inner_n = grid_of(n)
    frags, rows, width = inner_weights.shape[1:]
    share = momentum.shape[1]
    wide = max(1, min(share // 128 - 1, round(0.6 * share / 128))) * 128
    narrow = share - wide
    chunks = rows // CHUNK_ROWS
    bf, f32 = jnp.bfloat16, jnp.float32
    dma = pltpu.SemaphoreType.DMA

    def bufs(n1, n2, w):
        full = (chunks, n1, n2, CHUNK_ROWS, w)
        line = (chunks, n2, CHUNK_ROWS, w)
        return [pltpu.VMEM(s, bf) for s in (full, full, full, line, line)]

    def sems(n1, n2):
        one, two, both = (chunks, n1), (chunks, n2), (chunks, n1, n2)
        return [dma(s) for s in (one,) * 3 + (two,) * 6 + (both,) * 3]

    scratch = [
        pltpu.VMEM((2, CHUNK_ROWS, width), jnp.int32),
        pltpu.VMEM((chunks, CHUNK_ROWS, width), bf),
        pltpu.VMEM((chunks, CHUNK_ROWS, share), f32),
        pltpu.VMEM((CHUNK_ROWS, wide), f32),
        pltpu.VMEM((CHUNK_ROWS, narrow), f32),
        dma((chunks,)), dma((2,)), dma((chunks,)), dma,
        *bufs(inner_n, outer, wide), *bufs(outer, inner_n, narrow),
        *sems(inner_n, outer), *sems(outer, inner_n),
    ]
    anywhere = pl.BlockSpec(memory_space=pl.ANY)
    in_vmem = pl.BlockSpec(memory_space=pltpu.VMEM)
    in_smem = pl.BlockSpec(memory_space=pltpu.SMEM)
    held = pl.pallas_call(
        functools.partial(exchange_kernel, (outer, inner_n, chunks, share, wide)),
        out_shape=(
            pltpu.VMEM((frags, chunks, CHUNK_ROWS, width), bf),
            pltpu.VMEM((chunks, inner_n, outer, CHUNK_ROWS, wide), bf),
            pltpu.VMEM((chunks, outer, inner_n, CHUNK_ROWS, narrow), bf),
            pltpu.VMEM((chunks, CHUNK_ROWS, share), f32),
        ),
        in_specs=[in_smem] + [pl.BlockSpec(memory_space=pltpu.HBM)] * 4,
        out_specs=(in_vmem,) * 4,
        scratch_shapes=scratch,
        compiler_params=pltpu.CompilerParams(
            collective_id=0, has_side_effects=True, vmem_limit_bytes=EXCHANGE_VMEM
        ),
        name="exchange",
    )(
        fragment,
        inner_weights.reshape(1, frags, chunks, CHUNK_ROWS, width),
        snapshot.reshape(chunks, CHUNK_ROWS, width),
        momentum.reshape(chunks, CHUNK_ROWS, share),
        rand_bits.reshape(chunks, CHUNK_ROWS, width),
    )

    new_snapshot, new_momentum, new_inner = pl.pallas_call(
        finish_kernel,
        in_specs=[in_smem] + [in_vmem] * 4,
        out_specs=(anywhere,) * 3,
        out_shape=(
            jax.ShapeDtypeStruct((chunks, CHUNK_ROWS, width), bf),
            jax.ShapeDtypeStruct((chunks, CHUNK_ROWS, share), f32),
            jax.ShapeDtypeStruct((1, frags, chunks, CHUNK_ROWS, width), bf),
        ),
        scratch_shapes=[
            pltpu.VMEM((chunks, CHUNK_ROWS, width), bf),
            pltpu.VMEM((chunks, CHUNK_ROWS, width), bf),
            dma, dma((frags,)), dma((chunks,)), dma((chunks,)),
        ],
        compiler_params=pltpu.CompilerParams(vmem_limit_bytes=FINISH_VMEM),
        name="finish",
    )(fragment, *held)
    return new_snapshot.reshape(rows, width), new_momentum.reshape(rows, share), new_inner.reshape(inner_weights.shape)


def solution(mesh):
    placed = (
        P("replica", None, "fsdp", None),
        P("fsdp", None),
        P("fsdp", "replica"),
        P("replica", "fsdp", None),
        P(),
    )
    return jax.shard_map(
        body,
        mesh=mesh,
        in_specs=placed,
        out_specs=(P("fsdp", None), P("fsdp", "replica"), P("replica", None, "fsdp", None)),
        check_vma=False,
    )
```

```python
import functools

import jax
import jax.numpy as jnp
from jax import lax
from jax.experimental import pallas as pl
from jax.experimental.pallas import tpu as pltpu
from jax.sharding import PartitionSpec as P

momentum_coef = 0.9
outer_rate = 0.7
blend_keep = 0.5
grid_scale = 4.0
bit_levels = 4096.0
MESH = pl.DeviceIdType.MESH
CHUNK_ROWS = 32
OLDEST_FIRST = True
EXCHANGE_VMEM = 42 << 20
FINISH_VMEM = 10 << 20


def when(cond):
    if isinstance(cond, bool):
        return (lambda f: f()) if cond else (lambda f: None)
    return pl.when(cond)


def grid_of(n):
    inner = max(k for k in range(1, n + 1) if n % k == 0 and k * k <= n)
    return n // inner, inner


class Part:
    def __init__(self, bufs, sems, line1, line2, me, cols, width, draining):
        self.own, self.r1, self.l1, self.r2, self.l2, self.res = bufs
        (self.s1, self.sr1, self.sl1, self.s2, self.sr2, self.sl2,
         self.g2, self.g2r, self.g2l, self.g1, self.g1r, self.g1l) = sems
        (self.p1, self.n1, self.d1) = line1
        (self.p2, self.n2, self.d2) = line2
        self.me, self.cols, self.width = me, cols, width
        self.top = self.n1 + self.n2 - 2
        self.last = 2 * self.top
        self.draining = draining

    def send(self, src, dst, send_sem, recv_sem, delta):
        copy = pltpu.make_async_remote_copy(
            src_ref=src, dst_ref=dst, send_sem=send_sem, recv_sem=recv_sem,
            device_id={"replica": self.me + delta}, device_id_type=MESH,
        )
        if self.draining:
            copy.wait_send()
        else:
            copy.start()

    def arrive(self, dst, recv_sem):
        if not self.draining:
            pltpu.make_async_remote_copy(
                src_ref=dst, dst_ref=dst, send_sem=recv_sem, recv_sem=recv_sem,
                device_id={"replica": self.me}, device_id_type=MESH,
            ).wait_recv()

    def add1(self, c, q, recv):
        if not self.draining:
            for i in range(self.n2):
                self.own[c, q, i] = self.own[c, q, i] + recv[c, q, i]

    def add2(self, c, q, recv):
        if not self.draining:
            self.own[c, self.p1, q] = self.own[c, self.p1, q] + recv[c, q]

    def send1(self, c, q, right):
        recv, sem, delta = (self.r1, self.sr1, self.d1) if right else (self.l1, self.sl1, -self.d1)
        self.send(self.own.at[c, q], recv.at[c, q], self.s1.at[c, q], sem.at[c, q], delta)

    def send2(self, c, q, right):
        recv, sem, delta = (self.r2, self.sr2, self.d2) if right else (self.l2, self.sl2, -self.d2)
        self.send(self.own.at[c, self.p1, q], recv.at[c, q], self.s2.at[c, q], sem.at[c, q], delta)

    def gsend2(self, c, q, right):
        sem, delta = (self.g2r, self.d2) if right else (self.g2l, -self.d2)
        block = self.res.at[c, self.p1, q]
        self.send(block, block, sem.at[c, q], self.g2.at[c, q], delta)

    def gsend1(self, c, q1, q2, right):
        sem, delta = (self.g1r, self.d1) if right else (self.g1l, -self.d1)
        block = self.res.at[c, q1, q2]
        self.send(block, block, sem.at[c, q1, q2], self.g1.at[c, q1, q2], delta)

    def spread1(self, c, q2):
        p1 = self.p1
        when(p1 < self.n1 - 1)(lambda: self.gsend1(c, p1, q2, True))
        when(p1 > 0)(lambda: self.gsend1(c, p1, q2, False))

    def reduce_line(self, c, h, p, n, send, arrived, recvs, sems, add):
        right_recv, left_recv = recvs
        right_sem, left_sem = sems

        @when(p == h)
        def _():
            for q in range(n - 1, h - (h > 0), -1):
                if h > 0:
                    self.arrive(right_recv.at[c, q], right_sem.at[c, q])
                    if q > h or arrived:
                        add(c, q, right_recv)
                if q > h:
                    send(c, q, True)

        e = n - 1 - h

        @when(p == e)
        def _():
            for q in range(0, e + (h > 0)):
                if h > 0:
                    self.arrive(left_recv.at[c, q], left_sem.at[c, q])
                    if q < e or arrived:
                        add(c, q, left_recv)
                if q < e:
                    send(c, q, False)

    def hop1(self, s, c):
        if s < self.n1:
            self.reduce_line(c, s, self.p1, self.n1, self.send1, True, (self.r1, self.l1), (self.sr1, self.sl1), self.add1)

    def hop2(self, s, c):
        h = s - (self.n1 - 1)
        if 0 <= h < self.n2:
            self.reduce_line(c, h, self.p2, self.n2, self.send2, False, (self.r2, self.l2), (self.sr2, self.sl2), self.add2)

    def update(self, c, snap, mom, mom_next, acc, replicas, share):
        p1, p2 = self.p1, self.p2
        if not self.draining:
            acc[...] = self.own[c, p1, p2].astype(jnp.float32)

            @when(p2 > 0)
            def _():
                acc[...] += self.r2[c, p2].astype(jnp.float32)

            @when(p2 < self.n2 - 1)
            def _():
                acc[...] += self.l2[c, p2].astype(jnp.float32)

            start = self.me * share + self.cols
            if not isinstance(start, int):
                start = pl.multiple_of(start, 128)
            here = pl.ds(self.cols, self.width)
            grad = acc[...] / replicas
            moment = momentum_coef * mom[c, :, here] + grad
            mom_next[c, :, here] = moment
            base = snap[c, :, pl.ds(start, self.width)].astype(jnp.float32)
            self.res[c, p1, p2] = (base - outer_rate * (grad + momentum_coef * moment)).astype(jnp.bfloat16)
        when(p2 < self.n2 - 1)(lambda: self.gsend2(c, p2, True))
        when(p2 > 0)(lambda: self.gsend2(c, p2, False))
        self.spread1(c, p2)

    def gather(self, s, c):
        g = s - self.top
        p1, n1, p2, n2 = self.p1, self.n1, self.p2, self.n2
        if 1 <= g < n2:
            @when(p2 >= g)
            def _():
                self.arrive(self.res.at[c, p1, p2 - g], self.g2.at[c, p2 - g])
                when(p2 < n2 - 1)(lambda: self.gsend2(c, p2 - g, True))
                self.spread1(c, p2 - g)

            @when(p2 + g < n2)
            def _():
                self.arrive(self.res.at[c, p1, p2 + g], self.g2.at[c, p2 + g])
                when(p2 > 0)(lambda: self.gsend2(c, p2 + g, False))
                self.spread1(c, p2 + g)

        for h in range(n2):
            k = g - h
            if not 1 <= k < n1:
                continue
            for side in ((-1, 1) if h else (1,)):
                q2 = p2 + side * h

                @when(q2 >= 0 if side < 0 else q2 < n2)
                def _():
                    @when(p1 >= k)
                    def _():
                        self.arrive(self.res.at[c, p1 - k, q2], self.g1.at[c, p1 - k, q2])
                        when(p1 < n1 - 1)(lambda: self.gsend1(c, p1 - k, q2, True))

                    @when(p1 + k < n1)
                    def _():
                        self.arrive(self.res.at[c, p1 + k, q2], self.g1.at[c, p1 + k, q2])
                        when(p1 > 0)(lambda: self.gsend1(c, p1 + k, q2, False))


def exchange_kernel(dims, frag, inner, snapshot, momentum, bits, inner_v, res_a, res_b, mom_next, *scratch):
    outer, inner_n, chunks, share, wide = dims
    replicas = outer * inner_n
    frags = inner_v.shape[0]
    bbuf, snap, mom, acc_a, acc_b, wsem, bsem, ssem, msem = scratch[:9]
    bufs_a, bufs_b = (*scratch[9:14], res_a), (*scratch[14:19], res_b)
    sems_a, sems_b = scratch[19:31], scratch[31:43]
    me = lax.axis_index("replica")
    y, z = lax.rem(me, inner_n), lax.div(me, inner_n)
    line_y, line_z = (y, inner_n, 1), (z, outer, inner_n)

    def parts_at(r, draining):
        at_y, at_z = (r % inner_n, inner_n, 1), (r // inner_n, outer, inner_n)
        return (
            Part(bufs_a, sems_a, at_y, at_z, r, 0, wide, draining),
            Part(bufs_b, sems_b, at_z, at_y, r, wide, share - wide, draining),
        )

    def loads(c, slot):
        return (
            pltpu.make_async_copy(inner.at[0, :, c], inner_v.at[:, c], wsem.at[c]),
            pltpu.make_async_copy(bits.at[c], bbuf.at[slot], bsem.at[slot]),
            pltpu.make_async_copy(snapshot.at[c], snap.at[c], ssem.at[c]),
        )

    for copy in loads(0, 0):
        copy.start()
    mom_copy = pltpu.make_async_copy(momentum, mom, msem)
    mom_copy.start()

    barrier = pltpu.get_barrier_semaphore()
    count = 0
    for pos, n, step in (line_y, line_z):
        for delta, there in ((-step, pos > 0), (step, pos < n - 1)):
            @pl.when(there)
            def _():
                pl.semaphore_signal(barrier, inc=1, device_id={"replica": me + delta}, device_id_type=MESH)

            count = count + there.astype(jnp.int32)
    pl.semaphore_wait(barrier, count)
    mom_copy.wait()

    def round_chunk(c):
        slot = lax.rem(c, 2)

        @pl.when(c + 1 < chunks)
        def _():
            for copy in loads(c + 1, 1 - slot):
                copy.start()

        for copy in loads(c, slot):
            copy.wait()
        which = frag[0]
        for b in range(replicas):
            cols = slice(b * share, (b + 1) * share)
            chosen = inner_v[0, c, :, cols].astype(jnp.float32)
            for f in range(1, frags):
                chosen = jnp.where(which == f, inner_v[f, c, :, cols].astype(jnp.float32), chosen)
            scaled = grid_scale * (snap[c, :, cols].astype(jnp.float32) - chosen)
            lower = jnp.floor(scaled)
            raised = jnp.where(bbuf[slot, :, cols].astype(jnp.float32) < bit_levels * (scaled - lower), 1.0, 0.0)
            rounded = ((lower + raised) / grid_scale).astype(jnp.bfloat16)
            bz, by = b // inner_n, b % inner_n
            bufs_a[0][c, by, bz] = rounded[:, :wide]
            bufs_b[0][c, bz, by] = rounded[:, wide:]

    def stage(s, c, parts):
        for part in parts:
            part.hop1(s, c)
            part.hop2(s, c)
        if s == top:
            parts[0].update(c, snap, mom, mom_next, acc_a, replicas, share)
            parts[1].update(c, snap, mom, mom_next, acc_b, replicas, share)
        for part in parts:
            part.gather(s, c)

    top = inner_n + outer - 2
    stages = 2 * top + 1

    def at_my_place(todo, draining):
        for r in range(replicas):
            pl.when(me == r)(functools.partial(todo, parts_at(r, draining)))

    def tick(t, carry):
        def older(parts):
            for s in (range(stages - 1, 0, -1) if OLDEST_FIRST else range(1, stages)):
                c = t - s

                @pl.when(jnp.logical_and(c >= 0, c < chunks))
                def _():
                    stage(s, c, parts)

        if OLDEST_FIRST:
            at_my_place(older, False)

        @pl.when(t < chunks)
        def _():
            round_chunk(t)
            at_my_place(lambda parts: stage(0, t, parts), False)

        if not OLDEST_FIRST:
            at_my_place(older, False)
        return carry

    lax.fori_loop(0, chunks + stages - 1, tick, 0)

    def drain_at(parts):
        def drain(c, carry):
            for s in range(stages):
                stage(s, c, parts)
            return carry

        lax.fori_loop(0, chunks, drain, 0)

    at_my_place(drain_at, True)


def finish_kernel(frag, inner_v, res_a, res_b, mom_next, snap_out, mom_out, inner_out, snap_v, blend_v, mom_sem, pass_sem, snap_sem, blend_sem):
    frags, chunks = inner_v.shape[:2]
    n_y, n_z = res_a.shape[1], res_a.shape[2]
    wide = res_a.shape[4]
    share = wide + res_b.shape[4]
    which = frag[0]
    waits = [pltpu.make_async_copy(mom_next, mom_out, mom_sem)]
    for j in range(1, frags):
        other = lax.rem(which + j, frags)
        waits.append(pltpu.make_async_copy(inner_v.at[other], inner_out.at[0, other], pass_sem.at[j]))

    def puts(c):
        return (
            pltpu.make_async_copy(snap_v.at[c], snap_out.at[c], snap_sem.at[c]),
            pltpu.make_async_copy(blend_v.at[c], inner_out.at[0, which, c], blend_sem.at[c]),
        )

    for copy in waits:
        copy.start()

    def blend(c, carry):
        for bz in range(n_z):
            for by in range(n_y):
                first = (bz * n_y + by) * share
                for col, part in ((first, res_a[c, by, bz]), (first + wide, res_b[c, bz, by])):
                    cols = slice(col, col + part.shape[1])
                    snap_v[c, :, cols] = part
                    blend_v[c, :, cols] = (
                        blend_keep * inner_v[which, c, :, cols].astype(jnp.float32)
                        + (1.0 - blend_keep) * part.astype(jnp.float32)
                    ).astype(jnp.bfloat16)
        for copy in puts(c):
            copy.start()
        return carry

    lax.fori_loop(0, chunks, blend, 0)
    for copy in waits:
        copy.wait()

    def settle(c, carry):
        for copy in puts(c):
            copy.wait()
        return carry

    lax.fori_loop(0, chunks, settle, 0)


def body(inner_weights, snapshot, momentum, rand_bits, fragment):
    n = lax.axis_size("replica")
    outer, inner_n = grid_of(n)
    frags, rows, width = inner_weights.shape[1:]
    share = momentum.shape[1]
    wide = max(1, min(share // 128 - 1, round(0.6 * share / 128))) * 128
    narrow = share - wide
    chunks = rows // CHUNK_ROWS
    bf, f32 = jnp.bfloat16, jnp.float32
    dma = pltpu.SemaphoreType.DMA

    def bufs(n1, n2, w):
        full = (chunks, n1, n2, CHUNK_ROWS, w)
        line = (chunks, n2, CHUNK_ROWS, w)
        return [pltpu.VMEM(s, bf) for s in (full, full, full, line, line)]

    def sems(n1, n2):
        one, two, both = (chunks, n1), (chunks, n2), (chunks, n1, n2)
        return [dma(s) for s in (one,) * 3 + (two,) * 6 + (both,) * 3]

    scratch = [
        pltpu.VMEM((2, CHUNK_ROWS, width), jnp.int32),
        pltpu.VMEM((chunks, CHUNK_ROWS, width), bf),
        pltpu.VMEM((chunks, CHUNK_ROWS, share), f32),
        pltpu.VMEM((CHUNK_ROWS, wide), f32),
        pltpu.VMEM((CHUNK_ROWS, narrow), f32),
        dma((chunks,)), dma((2,)), dma((chunks,)), dma,
        *bufs(inner_n, outer, wide), *bufs(outer, inner_n, narrow),
        *sems(inner_n, outer), *sems(outer, inner_n),
    ]
    anywhere = pl.BlockSpec(memory_space=pl.ANY)
    in_vmem = pl.BlockSpec(memory_space=pltpu.VMEM)
    in_smem = pl.BlockSpec(memory_space=pltpu.SMEM)
    held = pl.pallas_call(
        functools.partial(exchange_kernel, (outer, inner_n, chunks, share, wide)),
        out_shape=(
            pltpu.VMEM((frags, chunks, CHUNK_ROWS, width), bf),
            pltpu.VMEM((chunks, inner_n, outer, CHUNK_ROWS, wide), bf),
            pltpu.VMEM((chunks, outer, inner_n, CHUNK_ROWS, narrow), bf),
            pltpu.VMEM((chunks, CHUNK_ROWS, share), f32),
        ),
        in_specs=[in_smem] + [pl.BlockSpec(memory_space=pltpu.HBM)] * 4,
        out_specs=(in_vmem,) * 4,
        scratch_shapes=scratch,
        compiler_params=pltpu.CompilerParams(
            collective_id=0, has_side_effects=True, vmem_limit_bytes=EXCHANGE_VMEM
        ),
        name="exchange",
    )(
        fragment,
        inner_weights.reshape(1, frags, chunks, CHUNK_ROWS, width),
        snapshot.reshape(chunks, CHUNK_ROWS, width),
        momentum.reshape(chunks, CHUNK_ROWS, share),
        rand_bits.reshape(chunks, CHUNK_ROWS, width),
    )

    new_snapshot, new_momentum, new_inner = pl.pallas_call(
        finish_kernel,
        in_specs=[in_smem] + [in_vmem] * 4,
        out_specs=(anywhere,) * 3,
        out_shape=(
            jax.ShapeDtypeStruct((chunks, CHUNK_ROWS, width), bf),
            jax.ShapeDtypeStruct((chunks, CHUNK_ROWS, share), f32),
            jax.ShapeDtypeStruct((1, frags, chunks, CHUNK_ROWS, width), bf),
        ),
        scratch_shapes=[
            pltpu.VMEM((chunks, CHUNK_ROWS, width), bf),
            pltpu.VMEM((chunks, CHUNK_ROWS, width), bf),
            dma, dma((frags,)), dma((chunks,)), dma((chunks,)),
        ],
        compiler_params=pltpu.CompilerParams(vmem_limit_bytes=FINISH_VMEM),
        name="finish",
    )(fragment, *held)
    return new_snapshot.reshape(rows, width), new_momentum.reshape(rows, share), new_inner.reshape(inner_weights.shape)


def solution(mesh):
    placed = (
        P("replica", None, "fsdp", None),
        P("fsdp", None),
        P("fsdp", "replica"),
        P("replica", "fsdp", None),
        P(),
    )
    return jax.shard_map(
        body,
        mesh=mesh,
        in_specs=placed,
        out_specs=(P("fsdp", None), P("fsdp", "replica"), P("replica", None, "fsdp", None)),
        check_vma=False,
    )
```
